32 devices in a mesh: adapter: 8 (over z, x), feature: 4 (over y, core).
Axes of the slice: x: 2, y: 2, z: 4, core: 2. Of those that a mesh axis runs over, the one named last changes fastest.
Arguments:
- adapter_down: bfloat16 [128, 16, 8192], P('adapter', None, 'feature'), may hold values from -6 to 6
- adapter_up: bfloat16 [128, 16, 8192], P('adapter', None, 'feature'), may hold values from -6 to 6
- fisher: float32 [128], P('adapter'), may hold values from 0.1 to 10
- init_v: float32 [8192, 64], P('feature'), may hold values from -0.0625 to 0.0625
- init_u: float32 [8192, 64], P('feature'), may hold values from -0.0625 to 0.0625
- prompt_rows: bfloat16 [4096, 8192], P('adapter', 'feature'), may hold values from -6 to 6
- request_ids: int32 [32], P('adapter'), may hold values from 0 to 127
Outputs:
- served: bfloat16 [4096, 8192], P('adapter', 'feature')
The draws below stay inside these ranges and needn't reach their ends.
All inputs are finite; a program needn't handle non-finite values.
Results may differ from the reference program's by a relative error of at most 0.025.
Values may be sent and summed in bfloat16 or wider, within the bound.
A program may use at most 64 MiB of HBM per device.

```python
import math
import jax
import jax.numpy as jnp
import numpy as np
from jax import lax

D = 8192
RANK = 16
BASIS = 64
SWEEPS = 3
BLOCK_ROWS = 128
ADAPTERS = 128
ROWS = 4096
BLOCKS = 32


def touch_ends(drawn, stream_key, low, top_value):
    longest = drawn.shape.index(max(drawn.shape))
    spots = []
    for shift in (0, 1):
        where = [jax.random.randint(jax.random.fold_in(stream_key, axis), (), 0, length) for axis, length in enumerate(drawn.shape)]
        where[longest] = (where[longest] + shift) % drawn.shape[longest]
        spots.append(tuple(where))
    return drawn.at[spots[0]].set(low).at[spots[1]].set(top_value)


def steps_of(rng, shape, split, smallest, top_value):
    def one(dim, shards_of):
        steps = jax.random.uniform(jax.random.fold_in(jax.random.fold_in(rng, 6), dim), (shards_of,), jnp.float32, smallest / len(split), top_value / len(split))
        return jnp.repeat(jnp.exp(steps), shape[dim] // shards_of).reshape((-1,) + (1,) * (len(shape) - dim - 1))

    level = one(*split[0])
    for cut in split[1:]:
        level = level * one(*cut)
    return level


def rank_bounds(number_of, skew):
    weights = [(1 << 20) // math.isqrt(grade ** skew) + 1 for grade in range(1, number_of + 1)]
    scale = 1 + sum(weights) // (1 << 30)
    return np.cumsum(np.array([max(1, weight // scale) for weight in weights]))


def ranked(stream_key, extent, number_of, slope):
    grid = rank_bounds(number_of, slope)
    lot = jax.random.randint(jax.random.fold_in(stream_key, 1), extent, 0, int(grid[number_of - 1]))
    grade = jnp.searchsorted(jnp.asarray(grid, jnp.int32), lot, side="right")
    return jax.random.permutation(jax.random.fold_in(stream_key, 2), number_of)[grade].astype(jnp.int32)


def gaussian(key, dims, scale, limit, shards=(), dtype=jnp.bfloat16):
    array = scale * jax.random.normal(key, dims, jnp.float32)
    if shards:
        array = array * steps_of(key, dims, shards, -0.22, 0.18)
    return jnp.clip(array, -limit, limit).astype(dtype)


def setup_inputs(seed: int = 0) -> dict:
    key_list = jax.random.split(jax.random.key(seed), 8)
    return {
        "adapter_down": gaussian(key_list[0], (ADAPTERS, RANK, D), 1.0, 6.0, ((0, 8), (2, 4))),
        "adapter_up": gaussian(key_list[1], (ADAPTERS, RANK, D), 1.0, 6.0, ((0, 8), (2, 4))),
        "fisher": jnp.clip(jnp.exp(math.log(10.0) - 4.6051702 * jax.random.uniform(key_list[2], (ADAPTERS,), jnp.float32) ** steps_of(key_list[2], (ADAPTERS,), ((0, 8),), -0.2, 0.2)), 0.1, 10.0),
        "init_v": gaussian(key_list[3], (D, BASIS), D ** -0.5, 0.0625, ((0, 4),), jnp.float32),
        "init_u": gaussian(key_list[4], (D, BASIS), D ** -0.5, 0.0625, ((0, 4),), jnp.float32),
        "prompt_rows": gaussian(key_list[5], (ROWS, D), 1.0, 6.0, ((0, 8), (1, 4))),
        "request_ids": touch_ends(ranked(key_list[6], (BLOCKS,), ADAPTERS, 2), jax.random.fold_in(key_list[6], 3), 0, ADAPTERS - 1).astype(jnp.int32),
    }


highest = lax.Precision.HIGHEST

def project(adapter_stack, basis_low):
    flat = adapter_stack.reshape(-1, adapter_stack.shape[-1])
    result = jnp.dot(flat.astype(jnp.float32), basis_low.astype(jnp.float32), preferred_element_type=jnp.float32)
    return result.reshape(adapter_stack.shape[0], adapter_stack.shape[1], -1)

def core_of(cols_q, rows_p):
    return jnp.einsum('irk,irl->ikl', cols_q, rows_p, precision=highest)

def numerator(adapter_stack, weighted):
    flat = adapter_stack.reshape(-1, adapter_stack.shape[-1])
    terms = weighted.reshape(-1, weighted.shape[-1])
    return lax.dot_general(flat.astype(jnp.float32), terms.astype(jnp.float32), (((0,), (0,)), ((), ())), preferred_element_type=jnp.float32)

def orthonormal(matrix):
    gram_sum = jnp.dot(matrix.T, matrix, precision=highest)
    factor = jnp.linalg.cholesky(gram_sum)
    return lax.linalg.triangular_solve(factor, matrix, left_side=False, lower=True, transpose_a=True)

def reference(adapter_down, adapter_up, fisher, init_v, init_u, prompt_rows, request_ids):
    basis_v = init_v
    basis_u = init_u
    weights = fisher[:, None, None]
    cols_q = project(adapter_up, basis_u.astype(jnp.bfloat16))
    for sweep_index in range(SWEEPS):
        rows_p = project(adapter_down, basis_v.astype(jnp.bfloat16))
        core_stack = core_of(cols_q, rows_p)
        weighted = (weights * jnp.einsum('irl,ikl->irk', rows_p, core_stack, precision=highest)).astype(jnp.bfloat16)
        basis_u = orthonormal(numerator(adapter_up, weighted))
        cols_q = project(adapter_up, basis_u.astype(jnp.bfloat16))
        core_stack = core_of(cols_q, rows_p)
        weighted = (weights * jnp.einsum('irk,ikl->irl', cols_q, core_stack, precision=highest)).astype(jnp.bfloat16)
        basis_v = orthonormal(numerator(adapter_down, weighted))
    rows_p = project(adapter_down, basis_v.astype(jnp.bfloat16))
    final_cores = core_of(cols_q, rows_p).astype(jnp.bfloat16)
    hidden = jnp.dot(prompt_rows.astype(jnp.float32), basis_v.astype(jnp.bfloat16).astype(jnp.float32), preferred_element_type=jnp.float32).astype(jnp.bfloat16)
    chosen = final_cores[request_ids.astype(jnp.int32)]
    blocked = hidden.reshape(BLOCKS, BLOCK_ROWS, BASIS)
    mixed_rows = jnp.einsum('bnl,bkl->bnk', blocked.astype(jnp.float32), chosen.astype(jnp.float32)).astype(jnp.bfloat16)
    served = jnp.dot(mixed_rows.reshape(ROWS, BASIS).astype(jnp.float32), basis_u.astype(jnp.bfloat16).T.astype(jnp.float32), preferred_element_type=jnp.float32)
    return served.astype(jnp.bfloat16)
```

```python
import functools

import jax
import jax.numpy as jnp
from jax import lax
from jax.experimental import pallas as pl
from jax.experimental.pallas import tpu as pltpu
from jax.sharding import PartitionSpec as P

SWEEPS = 3
GROUP = 8


highest = lax.Precision.HIGHEST


def dot32(left, right):
    return jnp.dot(left, right, precision=highest, preferred_element_type=jnp.float32)


def dot_nt(left, right):
    return lax.dot_general(
        left, right, (((1,), (1,)), ((), ())), preferred_element_type=jnp.float32
    )


def inverse_factor(gram):
    width = gram.shape[0]
    rows = lax.broadcasted_iota(jnp.int32, (width, width), 0)
    columns = lax.broadcasted_iota(jnp.int32, (width, width), 1)
    eye = (rows == columns).astype(jnp.float32)
    table = jnp.concatenate([gram, eye], axis=1)
    blocks = [table[at : at + GROUP] for at in range(0, width, GROUP)]
    inner = lax.broadcasted_iota(jnp.int32, (GROUP, 1), 0)
    for k in range(width):
        first, offset = divmod(k, GROUP)
        row = blocks[first][offset : offset + 1]
        scaled = row / row[:, k : k + 1]
        for b in range(first, len(blocks)):
            factor = blocks[b][:, k : k + 1]
            if b == first:
                factor = jnp.where(inner > offset, factor, 0.0)
            blocks[b] = blocks[b] - factor * scaled
    table = jnp.concatenate(blocks, axis=0)
    pivots = jnp.sum(table[:, :width] * eye, axis=1, keepdims=True)
    return table[:, width:] / jnp.sqrt(pivots)


def weigh(rank, fresh, other, weights):
    total = fresh.shape[1]
    step = 128 if total % 128 == 0 and 128 % rank == 0 else total
    same = (
        lax.broadcasted_iota(jnp.int32, (step, step), 0) // rank
        == lax.broadcasted_iota(jnp.int32, (step, step), 1) // rank
    )
    parts = []
    for at in range(0, total, step):
        piece = fresh[:, at : at + step]
        inner = jnp.where(same, dot32(piece.T, piece), 0.0)
        parts.append(dot32(other[:, at : at + step], inner))
    joined = parts[0] if len(parts) == 1 else jnp.concatenate(parts, axis=1)
    return (joined * weights).astype(jnp.bfloat16)


def first_kernel(rank, fresh_ref, other_ref, weights_ref, flat_ref, term_ref):
    low = weigh(rank, fresh_ref[...], other_ref[...], weights_ref[...])
    term_ref[...] = jnp.dot(low, flat_ref[...], preferred_element_type=jnp.float32)


def turn_kernel(rank, sums_ref, other_ref, weights_ref, flat_ref, inverse_ref, fresh_ref, term_ref):
    extent = fresh_ref.shape[1]
    inverse = inverse_factor(sums_ref[:, extent:])
    inverse_ref[...] = inverse
    fresh = dot32(inverse, sums_ref[:, :extent])
    fresh_ref[...] = fresh
    low = weigh(rank, fresh, other_ref[...], weights_ref[...])
    term_ref[...] = jnp.dot(low, flat_ref[...], preferred_element_type=jnp.float32)


def last_kernel(sums_ref, fresh_ref):
    extent = fresh_ref.shape[1]
    inverse = inverse_factor(sums_ref[:, extent:])
    fresh_ref[...] = dot32(inverse, sums_ref[:, :extent])


def gram_kernel(full_ref, *refs):
    full = full_ref[...]
    high = full.astype(jnp.bfloat16)
    low = (full - high.astype(jnp.float32)).astype(jnp.bfloat16)
    both = jnp.concatenate([high, low], axis=0)
    width = full.shape[0]
    *stacks, sums_ref = refs
    at = 0
    for stack in stacks:
        pair = dot_nt(both, stack[...])
        sums_ref[:, at : at + pair.shape[1]] = pair[:width] + pair[width:]
        at += pair.shape[1]
    quad = dot_nt(both, both)
    half = quad[:width] + quad[width:]
    sums_ref[:, at : at + width] = half[:, :width] + half[:, width:]


def call(body, shapes, *args):
    return pl.pallas_call(
        body,
        out_shape=[jax.ShapeDtypeStruct(shape, jnp.float32) for shape in shapes],
        compiler_params=pltpu.CompilerParams(vmem_limit_bytes=40 * 2**20),
    )(*args)


def on_device(adapter_down, adapter_up, fisher, init_v, init_u, prompt_rows, request_ids):
    count_local, rank, depth = adapter_up.shape
    width = init_v.shape[1]
    rows = count_local * rank
    down = adapter_down.reshape(rows, depth)
    up = adapter_up.reshape(rows, depth)
    weights = jnp.repeat(fisher, rank)[None, :]

    def start(basis, flat):
        return lax.dot_general(
            basis.astype(jnp.bfloat16),
            flat,
            (((0,), (1,)), ((), ())),
            preferred_element_type=jnp.float32,
        )

    def sums(full, *stacks):
        extent = sum(stack.shape[0] for stack in stacks)
        (partial,) = call(gram_kernel, [(width, extent + width)], full, *stacks)
        return lax.psum(partial, "feature")

    both = lax.psum(
        jnp.concatenate([start(init_v, down), start(init_u, up)], axis=1), "feature"
    )
    rows_p, cols_q = both[:, :rows], both[:, rows:]
    shape_term, shape_rows, shape_gram = (width, depth), (width, rows), (width, width)
    (term,) = call(
        functools.partial(first_kernel, rank), [shape_term], rows_p, cols_q, weights, up
    )
    turn = functools.partial(turn_kernel, rank)
    shapes = [shape_gram, shape_rows, shape_term]
    for sweep_index in range(SWEEPS):
        full_u = lax.psum(term, "adapter")
        total = sums(full_u, up)
        inverse_u, cols_q, term = call(turn, shapes, total, rows_p, weights, down)
        full_v = lax.psum(term, "adapter")
        if sweep_index < SWEEPS - 1:
            total = sums(full_v, down)
            _, rows_p, term = call(turn, shapes, total, cols_q, weights, up)
    total = sums(full_v, down, prompt_rows)
    (fresh,) = call(last_kernel, [(width, rows + prompt_rows.shape[0])], total)
    rows_p, hidden = fresh[:, :rows], fresh[:, rows:].astype(jnp.bfloat16)
    basis_u = dot32(inverse_u, full_u).astype(jnp.bfloat16)
    final_cores = jnp.einsum(
        "kir,lir->ikl",
        cols_q.reshape(width, count_local, rank),
        rows_p.reshape(width, count_local, rank),
        precision=highest,
    ).astype(jnp.bfloat16)
    flat_cores = final_cores.reshape(count_local, width * width)
    every_core = lax.all_gather(flat_cores, "adapter", axis=0, tiled=True)
    onehot = (
        request_ids[:, None] == jnp.arange(every_core.shape[0], dtype=jnp.int32)[None, :]
    ).astype(jnp.bfloat16)
    own_cores = jnp.dot(onehot, every_core, preferred_element_type=jnp.float32).astype(jnp.bfloat16)
    blocks = own_cores.shape[0]
    mixed = jnp.einsum(
        "lbn,bkl->bnk",
        hidden.reshape(width, blocks, -1),
        own_cores.reshape(blocks, width, width),
        preferred_element_type=jnp.float32,
    ).astype(jnp.bfloat16)
    served = jnp.dot(
        mixed.reshape(-1, width), basis_u, preferred_element_type=jnp.float32
    )
    return served.astype(jnp.bfloat16)


def solution(mesh):
    placed = (
        P("adapter", None, "feature"),
        P("adapter", None, "feature"),
        P("adapter"),
        P("feature", None),
        P("feature", None),
        P("adapter", "feature"),
        P("adapter"),
    )
    return jax.shard_map(
        on_device, mesh=mesh, in_specs=placed, out_specs=P("adapter", "feature"), check_vma=False
    )
```
